32 devices in a mesh: grp: 2 (over x), par: 8 (over z, y), ex: 2 (over core).
Axes of the slice: x: 2, y: 2, z: 4, core: 2. Of those that a mesh axis runs over, the one named last changes fastest.
Arguments:
- gradients: bfloat16 [512, 16384], P(('grp', 'ex'), 'par'), parts along dimension 0
- proj_seed: int32 [1], replicated, may hold values from 0 to 999999
- block_keys: int32 [1, 32], P(None, 'par'), may hold values from 0 to 999999
Outputs:
- features: bfloat16 [512, 8192], P(('grp', 'ex'), 'par'), parts along dimension 0
- kernel: float32 [512, 256], P(('grp', 'par'), 'ex'), parts along dimension 0
The draws below stay inside these ranges and needn't reach their ends.
There are 2 independent parts, one for each index of `grp`. The reference program is written for one: setup_inputs(seed, part) draws one part's arguments, and reference() takes and returns one part's arrays. A program takes and returns all parts, laid end to end along the dimension named above; an argument that names none is the same for every part. Nothing has to cross between parts.
All inputs are finite; a program needn't handle non-finite values.
Results may differ from the reference program's by a relative error of at most 0.01.
Values may be sent and summed in bfloat16 or wider, within the bound.
A program may use at most 64 MiB of HBM per device.

```python
import math
import jax
import jax.numpy as jnp
from jax import lax

K = 8192
PBLK = 512
P_DEV = 2048
P_SIZE = 16384
EXAMPLES = 256
NBLK = 32
N_PAR = 8


def draw_gradients(key, part):
    first, second, third = jax.random.split(key, 3)
    row_scale = jnp.exp(jax.random.uniform(first, (EXAMPLES, 1), jnp.float32, math.log(0.2), math.log(2.0)))
    col_scale = jnp.exp(jax.random.uniform(second, (1, P_SIZE), jnp.float32, math.log(0.3), math.log(3.0)))
    noise = jax.random.normal(third, (EXAMPLES, P_SIZE), jnp.float32)
    values = noise * row_scale * col_scale
    return values.astype(jnp.bfloat16)


def place_ends(values, key, least, high):
    place = [jax.random.randint(jax.random.fold_in(key, axis), (), 0, length) for axis, length in enumerate(values.shape)]
    longest = values.shape.index(max(values.shape))
    beside = place[:longest] + [(place[longest] + 1) % values.shape[longest]] + place[longest + 1:]
    return values.at[tuple(place)].set(least).at[tuple(beside)].set(high)


def setup_inputs(seed: int = 0, part: int = 0) -> dict:
    arg_keys = jax.random.split(jax.random.key(seed), 4)
    part_keys = jax.random.split(jax.random.fold_in(arg_keys[3], part), 4)
    gradients = draw_gradients(jax.random.fold_in(jax.random.fold_in(arg_keys[3], part), 71), part)
    proj_seed = jax.random.randint(arg_keys[1], (1,), 0, 1000000).astype(jnp.int32)
    block_keys = place_ends(jax.random.randint(arg_keys[2], (1, NBLK), 0, 1000000), jax.random.fold_in(arg_keys[2], 1), 0, 999999).astype(jnp.int32)
    return dict(gradients=gradients, proj_seed=proj_seed, block_keys=block_keys)


def rademacher(seed_value, block_key, row_index, col_index):
    mixed = row_index * 73856093 ^ col_index * 19349663 ^ block_key * 83492791 ^ seed_value
    mixed = mixed ^ mixed >> 13 & 524287
    mixed = mixed * 1540483477
    mixed = mixed ^ mixed >> 15 & 131071
    parity = mixed >> 11 & 1
    return (1 - 2 * parity).astype(jnp.bfloat16)

def reference(gradients, proj_seed, block_keys):
    examples = gradients.shape[0]
    block_count = P_DEV // PBLK
    seed_value = proj_seed[0]
    key_row = block_keys[0]
    local_rows = jnp.arange(PBLK, dtype=jnp.int32)[:, None]
    col_index = jnp.arange(K, dtype=jnp.int32)[None, :]

    def shard_step(summed, shard):

        def block_step(partial_value, number):
            base = (shard * P_DEV + number * PBLK).astype(jnp.int32)
            slab_part = lax.dynamic_slice_in_dim(gradients, base, PBLK, 1).astype(jnp.float32)
            block_key = lax.dynamic_slice_in_dim(key_row, (shard * block_count + number).astype(jnp.int32), 1)[0]
            sign_block = rademacher(seed_value, block_key, local_rows + base, col_index).astype(jnp.float32)
            return (partial_value + jnp.dot(slab_part, sign_block, precision=lax.Precision.HIGHEST), None)
        partial_value, _ = lax.scan(block_step, jnp.zeros((examples, K), jnp.float32), jnp.arange(block_count, dtype=jnp.int32))
        rounded = lax.optimization_barrier(partial_value.astype(jnp.bfloat16)).astype(jnp.float32)
        return (summed + rounded, None)
    projected, _ = lax.scan(shard_step, jnp.zeros((examples, K), jnp.float32), jnp.arange(N_PAR, dtype=jnp.int32))
    features = jnp.tanh(projected * (1.0 / math.sqrt(P_SIZE))).astype(jnp.bfloat16)
    kernel = jnp.dot(features, features.T, preferred_element_type=jnp.float32) * (1.0 / math.sqrt(K))
    return (features, kernel)
```

```python
import functools
import math

import jax
import jax.numpy as jnp
import numpy as np
from jax import lax
from jax.experimental import pallas as pl
from jax.experimental.pallas import tpu as pltpu
from jax.sharding import PartitionSpec as P

K = 8192
PBLK = 512
MESH = pl.DeviceIdType.MESH
ROW_MUL = 73856093
COL_MUL = 19349663
KEY_MUL = 83492791
MIX_MUL = int(np.array((1540483477 << 5) & 0xFFFFFFFF, np.uint32).astype(np.int32))

STEPS = 4
TILE = 256
CHUNKS = ((0, 16), (16, 16), (32, 32), (64, 32), (96, 32))
NC = len(CHUNKS)


def rademacher(seed_value, block_key, row_index, col_index):
    mixed = row_index * 73856093 ^ col_index * 19349663 ^ block_key * 83492791 ^ seed_value
    mixed = mixed ^ mixed >> 13 & 524287
    mixed = mixed * 1540483477
    mixed = mixed ^ mixed >> 15 & 131071
    parity = mixed >> 11 & 1
    return (1 - 2 * parity).astype(jnp.bfloat16)


def project(slab, key_row, row_base, seed_value, col_index):
    block_count = slab.shape[1] // PBLK
    local_rows = jnp.arange(PBLK, dtype=jnp.int32)[:, None]
    summed = None
    for number in range(block_count):
        sign_block = rademacher(
            seed_value, key_row[number], row_base + number * PBLK + local_rows, col_index
        )
        slab_part = slab[:, number * PBLK : (number + 1) * PBLK]
        product = jnp.dot(slab_part, sign_block, preferred_element_type=jnp.float32)
        summed = product if summed is None else summed + product
    return summed


def general(gradients, proj_seed, block_keys):
    local_params = gradients.shape[1]
    shard_count = lax.axis_size("par")
    shard_index = lax.axis_index("par")
    seed_value = proj_seed[0]
    all_cols = jnp.arange(K, dtype=jnp.int32)[None, :]
    partial_value = project(
        gradients, block_keys[0], shard_index * local_params, seed_value, all_cols
    )
    projected = lax.psum_scatter(
        partial_value.astype(jnp.bfloat16), "par", scatter_dimension=1, tiled=True
    ).astype(jnp.float32)
    features = jnp.tanh(projected * (1.0 / math.sqrt(local_params * shard_count))).astype(
        jnp.bfloat16
    )
    gathered = lax.all_gather(features, "ex", axis=0, tiled=True)
    product = lax.dot_general(
        gathered, features, (((1,), (1,)), ((), ())), preferred_element_type=jnp.float32
    )
    kernel = lax.psum_scatter(
        (product * (1.0 / math.sqrt(K))).astype(jnp.bfloat16),
        "par",
        scatter_dimension=0,
        tiled=True,
    ).astype(jnp.float32)
    return (features, kernel)


def fold(value):
    return value ^ lax.shift_right_logical(value, 13)


def line_kernel(
    seed_ref, key_ref, g_ref, feat_ref, kern_ref,
    x, signs, rows, keys, acc, yout, yin, zout, zin, feats, feats_in, kout, kin,
    load_sems, g_send, g_recv, c_send, c_recv, f_send, f_recv, key_sems,
    y_send, y_recv, z_send, z_recv, fx_send, fx_recv, k_send, k_recv, ready,
):
    ex_rows, params = g_ref.shape
    width = K // 16
    par, ex = lax.axis_index("par"), lax.axis_index("ex")
    z, y = par // 2, par % 2
    side, low = z // 2, z % 2
    other_y, other_ex, other_low = 1 - y, 1 - ex, 1 - low
    is_end = side == low
    is_mid = jnp.logical_not(is_end)
    me = par * 2 + ex
    blocks = params // PBLK

    half = jnp.where(is_end, side, 1 - side)
    z_cross = jnp.where(is_end, 1 + half, 3 * half)
    z_same = jnp.where(is_end, 3 * half, 1 + half)

    y_dev = {"par": z * 2 + other_y}
    c_dev = {"ex": other_ex}
    pair_dev = {"par": (side * 2 + other_low) * 2 + y}
    far_dev = {"par": (3 - z) * 2 + y}
    cross_dev = {"par": z_cross * 2 + y}

    barrier = pltpu.get_barrier_semaphore()
    pl.semaphore_signal(barrier, inc=1, device_id=y_dev, device_id_type=MESH)
    pl.semaphore_signal(barrier, inc=1, device_id=pair_dev, device_id_type=MESH)
    pl.semaphore_signal(barrier, inc=1, device_id=c_dev, device_id_type=MESH)

    @pl.when(is_mid)
    def _():
        pl.semaphore_signal(barrier, inc=1, device_id=far_dev, device_id_type=MESH)

    def remote(src, dst, send, recv, device):
        return pltpu.make_async_remote_copy(
            src_ref=src, dst_ref=dst, send_sem=send, recv_sem=recv,
            device_id=device, device_id_type=MESH,
        )

    def at_offset(k):
        target = lax.rem(me + k, 16)
        return {"par": target // 2, "ex": target % 2}

    def span(c):
        return slice(2 * CHUNKS[c][0], 2 * (CHUNKS[c][0] + CHUNKS[c][1]))

    def mine(c, core):
        first, count = CHUNKS[c]
        return pl.ds(pl.multiple_of(2 * first + core * count, 16), count)

    loads, g_copies, c_copies, f_copies = [], [], [], []
    for c, (first, count) in enumerate(CHUNKS):
        here = x.at[low, mine(c, ex)]
        there = x.at[other_low, mine(c, ex)]
        loads.append(
            pltpu.make_async_copy(g_ref.at[pl.ds(first, count)], here, load_sems.at[c])
        )
        g_copies.append(remote(here, here, g_send.at[c], g_recv.at[c], pair_dev))
        c_copies.append(remote(here, here, c_send.at[c], c_recv.at[c], c_dev))
        f_copies.append(remote(there, there, f_send.at[c], f_recv.at[c], c_dev))
        loads[c].start()

    for b in range(blocks):
        keys[low, b : b + 1, :] = jnp.full((1, 128), key_ref[0, b], jnp.int32)
    seed = seed_ref[0]

    def make_rows(which):
        for b in range(blocks):
            index = lax.broadcasted_iota(jnp.int32, (PBLK, 128), 0)
            index = index + (((side * 2 + which) * 2 + y) * params + b * PBLK)
            value = index * ROW_MUL ^ (keys[which, b : b + 1, :] * KEY_MUL ^ seed)
            rows[which, b * PBLK : (b + 1) * PBLK, :] = fold(value)

    def make_signs(step, which):
        owner = (z_cross if step < 2 else z_same) * 2 + (other_y if step % 2 == 0 else y)
        base = owner * (2 * width) + ex * width
        cols = []
        for j in range(width // 128):
            col = lax.broadcasted_iota(jnp.int32, (8, 128), 1) + (base + j * 128)
            cols.append(fold(col * COL_MUL)[:1])

        def body(i, carry):
            start = pl.multiple_of(i * TILE, TILE)
            row = rows[which, pl.ds(start, TILE), :]
            for j, col in enumerate(cols):
                mixed = (row ^ col) * MIX_MUL
                mixed = mixed ^ (mixed << 15)
                sign = jnp.where(mixed < 0, jnp.bfloat16(-1.0), jnp.bfloat16(1.0))
                signs[step, which, pl.ds(start, TILE), j * 128 : (j + 1) * 128] = sign
            return carry

        lax.fori_loop(0, params // TILE, body, 0)

    def multiply_own(s):
        left = x[low]
        for n in range(width // 256):
            cols = slice(n * 256, (n + 1) * 256)
            acc[s, :, cols] = jnp.dot(
                left, signs[s, low, :, cols], preferred_element_type=jnp.float32
            )

    def y_copy(c, kind):
        part = span(c)
        return remote(
            yout.at[kind, part], yin.at[kind, part],
            y_send.at[kind, c], y_recv.at[kind, c], y_dev,
        )

    def z_copy(c, kind):
        part = span(c)
        return remote(
            zout.at[kind, part], zin.at[kind, part], z_send.at[kind, c], z_recv.at[kind, c],
            cross_dev if kind == 0 else far_dev,
        )

    def multiply(first, last, s):
        part = slice(span(first).start, span(last).stop)
        left = x[other_low, part]
        for n in range(width // 256):
            cols = slice(n * 256, (n + 1) * 256)
            total = acc[s, part, cols] + jnp.dot(
                left, signs[s, other_low, :, cols], preferred_element_type=jnp.float32
            )
            if s % 2 == 0:
                yout[s // 2, part, cols] = total.astype(jnp.bfloat16)
            else:
                acc[s, part, cols] = total
        if s % 2 == 0:
            for c in range(first, last + 1):
                y_copy(c, s // 2).start()

    def combine(c, kind):
        part = span(c)
        y_copy(c, kind).wait_recv()
        total = acc[2 * kind + 1, part] + yin[kind, part].astype(jnp.float32)
        if kind == 0:
            zout[0, part] = total.astype(jnp.bfloat16)
            z_copy(c, 0).start()
            return

        @pl.when(is_mid)
        def _():
            zout[1, part] = total.astype(jnp.bfloat16)
            z_copy(c, 1).start()

        @pl.when(is_end)
        def _():
            acc[3, part] = total

    scale = 1.0 / math.sqrt(params * 8)

    def fx_copy(c):
        first, count = CHUNKS[c]
        part = pl.ds(first, count)
        return remote(
            feats.at[other_ex, part], feats_in.at[part], fx_send.at[c], fx_recv.at[c], c_dev
        )

    def settle(c):
        first, count = CHUNKS[c]
        part = span(c)
        z_copy(c, 0).wait_recv()

        @pl.when(is_mid)
        def _():
            z_copy(c, 1).wait_recv()
            acc[3, part] = zin[1, part].astype(jnp.float32)

        total = acc[3, part] + zin[0, part].astype(jnp.float32)
        value = jnp.tanh(total * scale).astype(jnp.bfloat16)
        feats[:, first : first + count, :] = value.reshape(2, count, width)
        fx_copy(c).start()

    def forward(c):
        g_copies[c].wait_recv()
        f_copies[c].start()

    make_rows(low)
    make_signs(0, low)
    for c in range(NC):
        loads[c].wait()

    @pl.when(is_end)
    def _():
        pl.semaphore_wait(barrier, 3)

    @pl.when(is_mid)
    def _():
        pl.semaphore_wait(barrier, 4)
        pl.semaphore_signal(ready, inc=1, device_id=far_dev, device_id_type=MESH)

    key_copy = remote(keys.at[low], keys.at[low], key_sems.at[0], key_sems.at[1], pair_dev)
    key_copy.start()
    for c in range(NC):
        g_copies[c].start()
    for c in range(NC):
        c_copies[c].start()

    make_signs(1, low)
    key_copy.wait_recv()
    make_rows(other_low)
    make_signs(0, other_low)
    for c in range(NC):
        c_copies[c].wait_recv()
    multiply_own(0)
    forward(0)
    make_signs(1, other_low)
    multiply_own(1)
    forward(1)
    f_copies[0].wait_recv()
    multiply(0, 0, 0)
    multiply(0, 0, 1)
    f_copies[1].wait_recv()
    multiply(1, 1, 0)
    multiply(1, 1, 1)
    make_signs(2, low)

    @pl.when(is_mid)
    def _():
        pl.semaphore_wait(ready, 1)

    combine(0, 0)
    combine(1, 0)
    forward(2)
    make_signs(2, other_low)
    multiply_own(2)
    multiply(0, 1, 2)
    f_copies[2].wait_recv()
    multiply(2, 2, 0)
    multiply(2, 2, 1)
    multiply(2, 2, 2)
    make_signs(3, low)
    forward(3)
    combine(2, 0)
    make_signs(3, other_low)
    multiply_own(3)
    multiply(0, 1, 3)
    combine(0, 1)
    combine(1, 1)
    f_copies[3].wait_recv()
    multiply(3, 3, 0)
    multiply(3, 3, 2)
    multiply(2, 2, 3)
    combine(2, 1)
    forward(4)
    multiply(3, 3, 1)
    multiply(3, 3, 3)
    combine(3, 0)
    f_copies[4].wait_recv()
    multiply(4, 4, 0)
    multiply(4, 4, 2)
    multiply(4, 4, 1)
    multiply(4, 4, 3)
    combine(3, 1)
    settle(0)
    settle(1)
    combine(4, 0)
    combine(4, 1)
    settle(2)
    settle(3)
    settle(4)

    whole = feats[...].reshape(2 * ex_rows, width)
    product = lax.dot_general(
        whole, whole, (((1,), (1,)), ((), ())), preferred_element_type=jnp.float32
    ) * (1.0 / math.sqrt(K))
    for half in range(2):
        columns = product[:, half * 128 : (half + 1) * 128].astype(jnp.bfloat16)
        kout[half] = columns.reshape(8, 32, 128)

    def k_copy(k):
        target = lax.rem(me + k, 16)
        return remote(
            kout.at[target % 2, target // 2], kin.at[k], k_send.at[k], k_recv.at[k], at_offset(k)
        )

    for k in range(1, 16):
        k_copy(k).start()
    feat_ref[:, pl.ds(pl.multiple_of(ex * width, width), width)] = feats[ex]
    for c in range(NC):
        fx_copy(c).wait_recv()
    feat_ref[:, pl.ds(pl.multiple_of(other_ex * width, width), width)] = feats_in[...]
    total = kout[ex, par].astype(jnp.float32)
    for k in range(1, 16):
        k_copy(k).wait_recv()
        total += kin[k].astype(jnp.float32)
    kern_ref[...] = total

    key_copy.wait_send()
    for c in range(NC):
        g_copies[c].wait_send()
        c_copies[c].wait_send()
        f_copies[c].wait_send()
        fx_copy(c).wait_send()
        y_copy(c, 0).wait_send()
        y_copy(c, 1).wait_send()
        z_copy(c, 0).wait_send()

    @pl.when(is_mid)
    def _():
        for c in range(NC):
            z_copy(c, 1).wait_send()

    for k in range(1, 16):
        k_copy(k).wait_send()


def write_kernel(feat_in, kern_in, feat_ref, kern_ref):
    feat_ref[...] = feat_in[...]
    kern_ref[...] = kern_in[...]


def line(gradients, proj_seed, block_keys):
    ex_rows, params = gradients.shape
    width = K // 16
    dma = pltpu.SemaphoreType.DMA
    bf16 = jnp.bfloat16
    pair = pl.pallas_call(
        line_kernel,
        out_shape=(
            jax.ShapeDtypeStruct((ex_rows, K // 8), bf16),
            jax.ShapeDtypeStruct((2 * ex_rows // 8, ex_rows), jnp.float32),
        ),
        in_specs=[
            pl.BlockSpec(memory_space=pltpu.SMEM),
            pl.BlockSpec(memory_space=pltpu.SMEM),
            pl.BlockSpec(memory_space=pl.ANY),
        ],
        out_specs=(
            pl.BlockSpec(memory_space=pltpu.VMEM),
            pl.BlockSpec(memory_space=pltpu.VMEM),
        ),
        scratch_shapes=[
            pltpu.VMEM((2, 2 * ex_rows, params), bf16),
            pltpu.VMEM((STEPS, 2, params, width), bf16),
            pltpu.VMEM((2, params, 128), jnp.int32),
            pltpu.VMEM((2, 8, 128), jnp.int32),
            pltpu.VMEM((STEPS, 2 * ex_rows, width), jnp.float32),
            pltpu.VMEM((2, 2 * ex_rows, width), bf16),
            pltpu.VMEM((2, 2 * ex_rows, width), bf16),
            pltpu.VMEM((2, 2 * ex_rows, width), bf16),
            pltpu.VMEM((2, 2 * ex_rows, width), bf16),
            pltpu.VMEM((2, ex_rows, width), bf16),
            pltpu.VMEM((ex_rows, width), bf16),
            pltpu.VMEM((2, 8, 32, 128), bf16),
            pltpu.VMEM((16, 32, 128), bf16),
            dma((NC,)), dma((NC,)), dma((NC,)), dma((NC,)), dma((NC,)), dma((NC,)), dma((NC,)),
            dma((2,)),
            dma((2, NC)), dma((2, NC)), dma((2, NC)), dma((2, NC)),
            dma((NC,)), dma((NC,)), dma((16,)), dma((16,)), pltpu.SemaphoreType.REGULAR,
        ],
        compiler_params=pltpu.CompilerParams(
            collective_id=0, has_side_effects=True, vmem_limit_bytes=56 * 1024 * 1024
        ),
    )(proj_seed, block_keys, gradients)
    return pl.pallas_call(
        write_kernel,
        out_shape=tuple(jax.ShapeDtypeStruct(part.shape, part.dtype) for part in pair),
    )(*pair)


def solution(mesh):
    placed = (P(("grp", "ex"), "par"), P(), P(None, "par"))
    special = mesh.shape["par"] == 8 and mesh.shape["ex"] == 2
    return jax.shard_map(
        line if special else general,
        mesh=mesh,
        in_specs=placed,
        out_specs=(P(("grp", "ex"), "par"), P(("grp", "par"), "ex")),
        check_vma=False,
    )
```

```python
import functools
import math

import jax
import jax.numpy as jnp
import numpy as np
from jax import lax
from jax.experimental import pallas as pl
from jax.experimental.pallas import tpu as pltpu
from jax.sharding import PartitionSpec as P

K = 8192
PBLK = 512
MESH = pl.DeviceIdType.MESH
ROW_MUL = 73856093
COL_MUL = 19349663
KEY_MUL = 83492791
MIX_MUL = int(np.array((1540483477 << 5) & 0xFFFFFFFF, np.uint32).astype(np.int32))

STEPS = 4
TILE = 256
CHUNKS = ((0, 16), (16, 32), (48, 32), (80, 32), (112, 16))
NC = len(CHUNKS)


def rademacher(seed_value, block_key, row_index, col_index):
    mixed = row_index * 73856093 ^ col_index * 19349663 ^ block_key * 83492791 ^ seed_value
    mixed = mixed ^ mixed >> 13 & 524287
    mixed = mixed * 1540483477
    mixed = mixed ^ mixed >> 15 & 131071
    parity = mixed >> 11 & 1
    return (1 - 2 * parity).astype(jnp.bfloat16)


def project(slab, key_row, row_base, seed_value, col_index):
    block_count = slab.shape[1] // PBLK
    local_rows = jnp.arange(PBLK, dtype=jnp.int32)[:, None]
    summed = None
    for number in range(block_count):
        sign_block = rademacher(
            seed_value, key_row[number], row_base + number * PBLK + local_rows, col_index
        )
        slab_part = slab[:, number * PBLK : (number + 1) * PBLK]
        product = jnp.dot(slab_part, sign_block, preferred_element_type=jnp.float32)
        summed = product if summed is None else summed + product
    return summed


def general(gradients, proj_seed, block_keys):
    local_params = gradients.shape[1]
    shard_count = lax.axis_size("par")
    shard_index = lax.axis_index("par")
    seed_value = proj_seed[0]
    all_cols = jnp.arange(K, dtype=jnp.int32)[None, :]
    partial_value = project(
        gradients, block_keys[0], shard_index * local_params, seed_value, all_cols
    )
    projected = lax.psum_scatter(
        partial_value.astype(jnp.bfloat16), "par", scatter_dimension=1, tiled=True
    ).astype(jnp.float32)
    features = jnp.tanh(projected * (1.0 / math.sqrt(local_params * shard_count))).astype(
        jnp.bfloat16
    )
    gathered = lax.all_gather(features, "ex", axis=0, tiled=True)
    product = lax.dot_general(
        gathered, features, (((1,), (1,)), ((), ())), preferred_element_type=jnp.float32
    )
    kernel = lax.psum_scatter(
        (product * (1.0 / math.sqrt(K))).astype(jnp.bfloat16),
        "par",
        scatter_dimension=0,
        tiled=True,
    ).astype(jnp.float32)
    return (features, kernel)


def fold(value):
    return value ^ lax.shift_right_logical(value, 13)


def line_kernel(
    seed_ref, key_hbm, g_ref, feat_ref, kern_ref,
    key_ref, x, signs, rows, keys, acc, yout, yin, zout, zin, feats, feats_in, kout, kin,
    scalar_sem, load_sems, g_send, g_recv, c_send, c_recv, f_send, f_recv, key_sems,
    y_send, y_recv, z_send, z_recv, fx_send, fx_recv, k_send, k_recv, ready,
):
    ex_rows, params = g_ref.shape
    width = K // 16
    par, ex = lax.axis_index("par"), lax.axis_index("ex")
    z, y = par // 2, par % 2
    side, low = z // 2, z % 2
    other_y, other_ex, other_low = 1 - y, 1 - ex, 1 - low
    is_end = side == low
    is_mid = jnp.logical_not(is_end)
    me = par * 2 + ex
    blocks = params // PBLK

    half = jnp.where(is_end, side, 1 - side)
    z_cross = jnp.where(is_end, 1 + half, 3 * half)
    z_same = jnp.where(is_end, 3 * half, 1 + half)

    y_dev = {"par": z * 2 + other_y}
    c_dev = {"ex": other_ex}
    pair_dev = {"par": (side * 2 + other_low) * 2 + y}
    far_dev = {"par": (3 - z) * 2 + y}
    cross_dev = {"par": z_cross * 2 + y}

    barrier = pltpu.get_barrier_semaphore()
    pl.semaphore_signal(barrier, inc=1, device_id=y_dev, device_id_type=MESH)
    pl.semaphore_signal(barrier, inc=1, device_id=pair_dev, device_id_type=MESH)
    pl.semaphore_signal(barrier, inc=1, device_id=c_dev, device_id_type=MESH)

    @pl.when(is_mid)
    def _():
        pl.semaphore_signal(barrier, inc=1, device_id=far_dev, device_id_type=MESH)

    scalars = pltpu.make_async_copy(key_hbm, key_ref, scalar_sem)
    scalars.start()

    def remote(src, dst, send, recv, device):
        return pltpu.make_async_remote_copy(
            src_ref=src, dst_ref=dst, send_sem=send, recv_sem=recv,
            device_id=device, device_id_type=MESH,
        )

    def at_offset(k):
        target = lax.rem(me + k, 16)
        return {"par": target // 2, "ex": target % 2}

    def span(c):
        return slice(2 * CHUNKS[c][0], 2 * (CHUNKS[c][0] + CHUNKS[c][1]))

    def mine(c, core):
        first, count = CHUNKS[c]
        return pl.ds(pl.multiple_of(2 * first + core * count, 16), count)

    loads, g_copies, c_copies, f_copies = [], [], [], []
    for c, (first, count) in enumerate(CHUNKS):
        here = x.at[low, mine(c, ex)]
        there = x.at[other_low, mine(c, ex)]
        loads.append(
            pltpu.make_async_copy(g_ref.at[pl.ds(first, count)], here, load_sems.at[c])
        )
        g_copies.append(remote(here, here, g_send.at[c], g_recv.at[c], pair_dev))
        c_copies.append(remote(here, here, c_send.at[c], c_recv.at[c], c_dev))
        f_copies.append(remote(there, there, f_send.at[c], f_recv.at[c], c_dev))
        loads[c].start()

    scalars.wait()
    for b in range(blocks):
        keys[low, b : b + 1, :] = jnp.full((1, 128), key_ref[0, b], jnp.int32)
    seed = seed_ref[0]

    def make_rows(which):
        for b in range(blocks):
            index = lax.broadcasted_iota(jnp.int32, (PBLK, 128), 0)
            index = index + (((side * 2 + which) * 2 + y) * params + b * PBLK)
            value = index * ROW_MUL ^ (keys[which, b : b + 1, :] * KEY_MUL ^ seed)
            rows[which, b * PBLK : (b + 1) * PBLK, :] = fold(value)

    def make_signs(step, which):
        owner = (z_same if step < 2 else z_cross) * 2 + (other_y if step % 2 == 0 else y)
        base = owner * (2 * width) + ex * width
        cols = []
        for j in range(width // 128):
            col = lax.broadcasted_iota(jnp.int32, (8, 128), 1) + (base + j * 128)
            cols.append(fold(col * COL_MUL)[:1])

        def body(i, carry):
            start = pl.multiple_of(i * TILE, TILE)
            row = rows[which, pl.ds(start, TILE), :]
            for j, col in enumerate(cols):
                mixed = (row ^ col) * MIX_MUL
                mixed = mixed ^ (mixed << 15)
                sign = jnp.where(mixed < 0, jnp.bfloat16(-1.0), jnp.bfloat16(1.0))
                signs[step, which, pl.ds(start, TILE), j * 128 : (j + 1) * 128] = sign
            return carry

        lax.fori_loop(0, params // TILE, body, 0)

    def multiply_own(s):
        left = x[low]
        for n in range(width // 256):
            cols = slice(n * 256, (n + 1) * 256)
            acc[s, :, cols] = jnp.dot(
                left, signs[s, low, :, cols], preferred_element_type=jnp.float32
            )

    def y_copy(c, kind):
        part = span(c)
        return remote(
            yout.at[kind, part], yin.at[kind, part],
            y_send.at[kind, c], y_recv.at[kind, c], y_dev,
        )

    def z_copy(c, kind):
        part = span(c)
        return remote(
            zout.at[kind, part], zin.at[kind, part], z_send.at[kind, c], z_recv.at[kind, c],
            far_dev if kind == 0 else cross_dev,
        )

    def multiply(first, last, s):
        part = slice(span(first).start, span(last).stop)
        left = x[other_low, part]
        for n in range(width // 256):
            cols = slice(n * 256, (n + 1) * 256)
            total = acc[s, part, cols] + jnp.dot(
                left, signs[s, other_low, :, cols], preferred_element_type=jnp.float32
            )
            if s % 2 == 0:
                yout[s // 2, part, cols] = total.astype(jnp.bfloat16)
            else:
                acc[s, part, cols] = total
        if s % 2 == 0:
            for c in range(first, last + 1):
                y_copy(c, s // 2).start()

    def combine(c, kind):
        part = span(c)
        y_copy(c, kind).wait_recv()
        total = acc[2 * kind + 1, part] + yin[kind, part].astype(jnp.float32)
        if kind == 1:
            zout[1, part] = total.astype(jnp.bfloat16)
            z_copy(c, 1).start()
            return

        @pl.when(is_mid)
        def _():
            zout[0, part] = total.astype(jnp.bfloat16)
            z_copy(c, 0).start()

        @pl.when(is_end)
        def _():
            acc[1, part] = total

    scale = 1.0 / math.sqrt(params * 8)

    def fx_copy(c):
        first, count = CHUNKS[c]
        part = pl.ds(first, count)
        return remote(
            feats.at[other_ex, part], feats_in.at[part], fx_send.at[c], fx_recv.at[c], c_dev
        )

    def settle(c):
        first, count = CHUNKS[c]
        part = span(c)
        @pl.when(is_mid)
        def _():
            z_copy(c, 0).wait_recv()
            acc[1, part] = zin[0, part].astype(jnp.float32)

        z_copy(c, 1).wait_recv()
        total = acc[1, part] + zin[1, part].astype(jnp.float32)
        value = jnp.tanh(total * scale).astype(jnp.bfloat16)
        feats[:, first : first + count, :] = value.reshape(2, count, width)
        fx_copy(c).start()

    def forward(c):
        g_copies[c].wait_recv()
        f_copies[c].start()

    make_rows(low)
    for c in range(NC):
        loads[c].wait()

    @pl.when(is_end)
    def _():
        pl.semaphore_wait(barrier, 3)

    @pl.when(is_mid)
    def _():
        pl.semaphore_wait(barrier, 4)
        pl.semaphore_signal(ready, inc=1, device_id=far_dev, device_id_type=MESH)

    key_copy = remote(keys.at[low], keys.at[low], key_sems.at[0], key_sems.at[1], pair_dev)
    key_copy.start()
    for c in range(NC):
        g_copies[c].start()
    for c in range(NC):
        c_copies[c].start()

    make_signs(0, low)
    make_signs(1, low)
    key_copy.wait_recv()
    make_rows(other_low)
    make_signs(0, other_low)
    for c in range(NC):
        c_copies[c].wait_recv()
    forward(0)
    multiply_own(0)
    make_signs(1, other_low)
    f_copies[0].wait_recv()
    multiply(0, 0, 0)
    multiply_own(1)
    multiply(0, 0, 1)
    make_signs(2, low)
    forward(1)
    make_signs(2, other_low)
    f_copies[1].wait_recv()
    multiply(1, 1, 0)
    multiply(1, 1, 1)
    combine(0, 0)
    multiply_own(2)
    multiply(0, 1, 2)
    make_signs(3, low)
    forward(2)
    combine(1, 0)
    make_signs(3, other_low)
    f_copies[2].wait_recv()
    multiply(2, 2, 0)
    multiply(2, 2, 2)
    multiply(2, 2, 1)
    multiply_own(3)
    forward(3)
    multiply(0, 2, 3)

    @pl.when(is_mid)
    def _():
        pl.semaphore_wait(ready, 1)

    combine(2, 0)
    combine(0, 1)
    combine(1, 1)
    f_copies[3].wait_recv()
    multiply(3, 3, 2)
    multiply(3, 3, 0)
    multiply(3, 3, 3)
    multiply(3, 3, 1)
    forward(4)
    combine(2, 1)
    f_copies[4].wait_recv()
    multiply(4, 4, 2)
    multiply(4, 4, 0)
    multiply(4, 4, 3)
    multiply(4, 4, 1)
    combine(3, 1)
    combine(3, 0)
    settle(0)
    combine(4, 1)
    combine(4, 0)
    settle(1)
    settle(2)
    settle(3)
    settle(4)

    whole = feats[...].reshape(2 * ex_rows, width)
    product = lax.dot_general(
        whole, whole, (((1,), (1,)), ((), ())), preferred_element_type=jnp.float32
    ) * (1.0 / math.sqrt(K))
    for half in range(2):
        columns = product[:, half * 128 : (half + 1) * 128].astype(jnp.bfloat16)
        kout[half] = columns.reshape(8, 32, 128)

    def k_copy(k):
        target = lax.rem(me + k, 16)
        return remote(
            kout.at[target % 2, target // 2], kin.at[k], k_send.at[k], k_recv.at[k], at_offset(k)
        )

    for k in range(1, 16):
        k_copy(k).start()
    feat_ref[:, pl.ds(pl.multiple_of(ex * width, width), width)] = feats[ex]
    for c in range(NC):
        fx_copy(c).wait_recv()
    feat_ref[:, pl.ds(pl.multiple_of(other_ex * width, width), width)] = feats_in[...]
    total = kout[ex, par].astype(jnp.float32)
    for k in range(1, 16):
        k_copy(k).wait_recv()
        total += kin[k].astype(jnp.float32)
    kern_ref[...] = total

    key_copy.wait_send()
    for c in range(NC):
        g_copies[c].wait_send()
        c_copies[c].wait_send()
        f_copies[c].wait_send()
        fx_copy(c).wait_send()
        y_copy(c, 0).wait_send()
        y_copy(c, 1).wait_send()
        z_copy(c, 1).wait_send()

    @pl.when(is_mid)
    def _():
        for c in range(NC):
            z_copy(c, 0).wait_send()

    for k in range(1, 16):
        k_copy(k).wait_send()


def write_kernel(feat_in, kern_in, feat_ref, kern_ref, sems):
    copies = (
        pltpu.make_async_copy(feat_in, feat_ref, sems.at[0]),
        pltpu.make_async_copy(kern_in, kern_ref, sems.at[1]),
    )
    for copy in copies:
        copy.start()
    for copy in copies:
        copy.wait()


def line(gradients, proj_seed, block_keys):
    ex_rows, params = gradients.shape
    width = K // 16
    dma = pltpu.SemaphoreType.DMA
    bf16 = jnp.bfloat16
    pair = pl.pallas_call(
        line_kernel,
        out_shape=(
            jax.ShapeDtypeStruct((ex_rows, K // 8), bf16),
            jax.ShapeDtypeStruct((2 * ex_rows // 8, ex_rows), jnp.float32),
        ),
        in_specs=[
            pl.BlockSpec(memory_space=pltpu.SMEM),
            pl.BlockSpec(memory_space=pltpu.HBM),
            pl.BlockSpec(memory_space=pltpu.HBM),
        ],
        out_specs=(
            pl.BlockSpec(memory_space=pltpu.VMEM),
            pl.BlockSpec(memory_space=pltpu.VMEM),
        ),
        scratch_shapes=[
            pltpu.SMEM(block_keys.shape, jnp.int32),
            pltpu.VMEM((2, 2 * ex_rows, params), bf16),
            pltpu.VMEM((STEPS, 2, params, width), bf16),
            pltpu.VMEM((2, params, 128), jnp.int32),
            pltpu.VMEM((2, 8, 128), jnp.int32),
            pltpu.VMEM((STEPS, 2 * ex_rows, width), jnp.float32),
            pltpu.VMEM((2, 2 * ex_rows, width), bf16),
            pltpu.VMEM((2, 2 * ex_rows, width), bf16),
            pltpu.VMEM((2, 2 * ex_rows, width), bf16),
            pltpu.VMEM((2, 2 * ex_rows, width), bf16),
            pltpu.VMEM((2, ex_rows, width), bf16),
            pltpu.VMEM((ex_rows, width), bf16),
            pltpu.VMEM((2, 8, 32, 128), bf16),
            pltpu.VMEM((16, 32, 128), bf16),
            dma, dma((NC,)),
            dma((NC,)), dma((NC,)), dma((NC,)), dma((NC,)), dma((NC,)), dma((NC,)),
            dma((2,)),
            dma((2, NC)), dma((2, NC)), dma((2, NC)), dma((2, NC)),
            dma((NC,)), dma((NC,)), dma((16,)), dma((16,)), pltpu.SemaphoreType.REGULAR,
        ],
        compiler_params=pltpu.CompilerParams(
            collective_id=0, has_side_effects=True, vmem_limit_bytes=30 * 1024 * 1024
        ),
    )(proj_seed, *(pltpu.with_memory_space_constraint(a, pltpu.HBM) for a in (block_keys, gradients)))
    return pl.pallas_call(
        write_kernel,
        out_shape=tuple(jax.ShapeDtypeStruct(part.shape, part.dtype) for part in pair),
        in_specs=[pl.BlockSpec(memory_space=pltpu.VMEM)] * 2,
        out_specs=(pl.BlockSpec(memory_space=pltpu.HBM),) * 2,
        scratch_shapes=[dma((2,))],
        compiler_params=pltpu.CompilerParams(vmem_limit_bytes=1024 * 1024),
    )(*pair)


def solution(mesh):
    placed = (P(("grp", "ex"), "par"), P(), P(None, "par"))
    special = mesh.shape["par"] == 8 and mesh.shape["ex"] == 2
    return jax.shard_map(
        line if special else general,
        mesh=mesh,
        in_specs=placed,
        out_specs=(P(("grp", "ex"), "par"), P(("grp", "par"), "ex")),
        check_vma=False,
    )
```

```python
import functools
import math

import jax
import jax.numpy as jnp
import numpy as np
from jax import lax
from jax.experimental import pallas as pl
from jax.experimental.pallas import tpu as pltpu
from jax.sharding import PartitionSpec as P

K = 8192
PBLK = 512
MESH = pl.DeviceIdType.MESH
ROW_MUL = 73856093
COL_MUL = 19349663
KEY_MUL = 83492791
MIX_MUL = int(np.array((1540483477 << 5) & 0xFFFFFFFF, np.uint32).astype(np.int32))

STEPS = 4
TILE = 256
CHUNKS = ((0, 16), (16, 48), (64, 32), (96, 16), (112, 16))
NC = len(CHUNKS)


def rademacher(seed_value, block_key, row_index, col_index):
    mixed = row_index * 73856093 ^ col_index * 19349663 ^ block_key * 83492791 ^ seed_value
    mixed = mixed ^ mixed >> 13 & 524287
    mixed = mixed * 1540483477
    mixed = mixed ^ mixed >> 15 & 131071
    parity = mixed >> 11 & 1
    return (1 - 2 * parity).astype(jnp.bfloat16)


def project(slab, key_row, row_base, seed_value, col_index):
    block_count = slab.shape[1] // PBLK
    local_rows = jnp.arange(PBLK, dtype=jnp.int32)[:, None]
    summed = None
    for number in range(block_count):
        sign_block = rademacher(
            seed_value, key_row[number], row_base + number * PBLK + local_rows, col_index
        )
        slab_part = slab[:, number * PBLK : (number + 1) * PBLK]
        product = jnp.dot(slab_part, sign_block, preferred_element_type=jnp.float32)
        summed = product if summed is None else summed + product
    return summed


def general(gradients, proj_seed, block_keys):
    local_params = gradients.shape[1]
    shard_count = lax.axis_size("par")
    shard_index = lax.axis_index("par")
    seed_value = proj_seed[0]
    all_cols = jnp.arange(K, dtype=jnp.int32)[None, :]
    partial_value = project(
        gradients, block_keys[0], shard_index * local_params, seed_value, all_cols
    )
    projected = lax.psum_scatter(
        partial_value.astype(jnp.bfloat16), "par", scatter_dimension=1, tiled=True
    ).astype(jnp.float32)
    features = jnp.tanh(projected * (1.0 / math.sqrt(local_params * shard_count))).astype(
        jnp.bfloat16
    )
    gathered = lax.all_gather(features, "ex", axis=0, tiled=True)
    product = lax.dot_general(
        gathered, features, (((1,), (1,)), ((), ())), preferred_element_type=jnp.float32
    )
    kernel = lax.psum_scatter(
        (product * (1.0 / math.sqrt(K))).astype(jnp.bfloat16),
        "par",
        scatter_dimension=0,
        tiled=True,
    ).astype(jnp.float32)
    return (features, kernel)


def fold(value):
    return value ^ lax.shift_right_logical(value, 13)


def line_kernel(
    seed_ref, key_hbm, g_ref, feat_ref, kern_ref,
    x, signs, rows, keys, acc, yout, yin, zout, zin, feats, feats_in, kout, kin,
    load_sems, g_send, g_recv, c_send, c_recv, f_send, f_recv, key_sems,
    y_send, y_recv, z_send, z_recv, fx_send, fx_recv, k_send, k_recv, ready,
):
    ex_rows, params = g_ref.shape
    width = K // 16
    par, ex = lax.axis_index("par"), lax.axis_index("ex")
    z, y = par // 2, par % 2
    side, low = z // 2, z % 2
    other_y, other_ex, other_low = 1 - y, 1 - ex, 1 - low
    is_end = side == low
    is_mid = jnp.logical_not(is_end)
    me = par * 2 + ex
    blocks = params // PBLK

    half = jnp.where(is_end, side, 1 - side)
    z_cross = jnp.where(is_end, 1 + half, 3 * half)
    z_same = jnp.where(is_end, 3 * half, 1 + half)

    y_dev = {"par": z * 2 + other_y}
    c_dev = {"ex": other_ex}
    pair_dev = {"par": (side * 2 + other_low) * 2 + y}
    far_dev = {"par": (3 - z) * 2 + y}
    cross_dev = {"par": z_cross * 2 + y}

    barrier = pltpu.get_barrier_semaphore()
    pl.semaphore_signal(barrier, inc=1, device_id=y_dev, device_id_type=MESH)
    pl.semaphore_signal(barrier, inc=1, device_id=pair_dev, device_id_type=MESH)
    pl.semaphore_signal(barrier, inc=1, device_id=c_dev, device_id_type=MESH)

    @pl.when(is_mid)
    def _():
        pl.semaphore_signal(barrier, inc=1, device_id=far_dev, device_id_type=MESH)


    def remote(src, dst, send, recv, device):
        return pltpu.make_async_remote_copy(
            src_ref=src, dst_ref=dst, send_sem=send, recv_sem=recv,
            device_id=device, device_id_type=MESH,
        )

    def at_offset(k):
        target = lax.rem(me + k, 16)
        return {"par": target // 2, "ex": target % 2}

    def span(c):
        return slice(2 * CHUNKS[c][0], 2 * (CHUNKS[c][0] + CHUNKS[c][1]))

    def mine(c, core):
        first, count = CHUNKS[c]
        return pl.ds(pl.multiple_of(2 * first + core * count, 16), count)

    loads, g_copies, c_copies, f_copies = [], [], [], []
    for c, (first, count) in enumerate(CHUNKS):
        own = g_ref.at[pl.ds(first, count)]
        here = x.at[low, mine(c, ex)]
        there = x.at[other_low, mine(c, ex)]
        loads.append(
            pltpu.make_async_copy(own, here, load_sems.at[c])
        )
        g_copies.append(remote(here, here, g_send.at[c], g_recv.at[c], pair_dev))
        c_copies.append(remote(here, here, c_send.at[c], c_recv.at[c], c_dev))
        f_copies.append(remote(there, there, f_send.at[c], f_recv.at[c], c_dev))
        loads[c].start()

    local_keys = pltpu.make_async_copy(key_hbm, keys.at[low], key_sems.at[2])
    local_keys.start()
    seed = seed_ref[0]

    def make_rows(which):
        for b in range(blocks):
            index = lax.broadcasted_iota(jnp.int32, (PBLK, 128), 0)
            index = index + (((side * 2 + which) * 2 + y) * params + b * PBLK)
            value = index * ROW_MUL ^ (keys[which, :, b : b + 1] * KEY_MUL ^ seed)
            rows[which, b * PBLK : (b + 1) * PBLK, :] = fold(value)

    def make_signs(step, which):
        owner = (z_same if step < 2 else z_cross) * 2 + (other_y if step % 2 == 0 else y)
        base = owner * (2 * width) + ex * width
        cols = []
        for j in range(width // 128):
            col = lax.broadcasted_iota(jnp.int32, (8, 128), 1) + (base + j * 128)
            cols.append(fold(col * COL_MUL)[:1])

        def body(i, carry):
            start = pl.multiple_of(i * TILE, TILE)
            row = rows[which, pl.ds(start, TILE), :]
            for j, col in enumerate(cols):
                mixed = (row ^ col) * MIX_MUL
                mixed = mixed ^ (mixed << 15)
                sign = jnp.where(mixed < 0, jnp.bfloat16(-1.0), jnp.bfloat16(1.0))
                signs[step, which, pl.ds(start, TILE), j * 128 : (j + 1) * 128] = sign
            return carry

        lax.fori_loop(0, params // TILE, body, 0)

    def multiply_own(s):
        left = x[low]
        for n in range(width // 256):
            cols = slice(n * 256, (n + 1) * 256)
            acc[s, :, cols] = jnp.dot(
                left, signs[s, low, :, cols], preferred_element_type=jnp.float32
            )

    def y_copy(c, kind):
        part = span(c)
        return remote(
            yout.at[kind, part], yin.at[kind, part],
            y_send.at[kind, c], y_recv.at[kind, c], y_dev,
        )

    def z_copy(c, kind):
        part = span(c)
        return remote(
            zout.at[kind, part], zin.at[kind, part], z_send.at[kind, c], z_recv.at[kind, c],
            far_dev if kind == 0 else cross_dev,
        )

    def multiply(first, last, s):
        part = slice(span(first).start, span(last).stop)
        left = x[other_low, part]
        for n in range(width // 256):
            cols = slice(n * 256, (n + 1) * 256)
            total = acc[s, part, cols] + jnp.dot(
                left, signs[s, other_low, :, cols], preferred_element_type=jnp.float32
            )
            if s % 2 == 0:
                yout[s // 2, part, cols] = total.astype(jnp.bfloat16)
            else:
                acc[s, part, cols] = total
        if s % 2 == 0:
            for c in range(first, last + 1):
                y_copy(c, s // 2).start()

    def combine(c, kind):
        part = span(c)
        y_copy(c, kind).wait_recv()
        total = acc[2 * kind + 1, part] + yin[kind, part].astype(jnp.float32)
        if kind == 1:
            zout[1, part] = total.astype(jnp.bfloat16)
            z_copy(c, 1).start()
            return

        @pl.when(is_mid)
        def _():
            zout[0, part] = total.astype(jnp.bfloat16)
            z_copy(c, 0).start()

        @pl.when(is_end)
        def _():
            acc[1, part] = total

    scale = 1.0 / math.sqrt(params * 8)

    def fx_copy(c):
        first, count = CHUNKS[c]
        part = pl.ds(first, count)
        return remote(
            feats.at[other_ex, part], feats_in.at[part], fx_send.at[c], fx_recv.at[c], c_dev
        )

    def settle(c):
        first, count = CHUNKS[c]
        part = span(c)
        @pl.when(is_mid)
        def _():
            z_copy(c, 0).wait_recv()
            acc[1, part] = zin[0, part].astype(jnp.float32)

        z_copy(c, 1).wait_recv()
        total = acc[1, part] + zin[1, part].astype(jnp.float32)
        value = jnp.tanh(total * scale).astype(jnp.bfloat16)
        feats[:, first : first + count, :] = value.reshape(2, count, width)
        fx_copy(c).start()

    def forward(c):
        g_copies[c].wait_recv()
        f_copies[c].start()

    for c in range(NC):
        loads[c].wait()

    @pl.when(is_end)
    def _():
        pl.semaphore_wait(barrier, 3)

    @pl.when(is_mid)
    def _():
        pl.semaphore_wait(barrier, 4)

    key_copy = remote(key_hbm, keys.at[low], key_sems.at[0], key_sems.at[1], pair_dev)
    key_copy.start()
    for c in range(NC):
        g_copies[c].start()
    for c in range(NC):
        c_copies[c].start()

    @pl.when(is_mid)
    def _():
        pl.semaphore_signal(ready, inc=1, device_id=far_dev, device_id_type=MESH)

    local_keys.wait()
    make_rows(low)
    make_signs(0, low)
    make_signs(1, low)
    key_copy.wait_recv()
    make_rows(other_low)
    make_signs(0, other_low)
    forward(0)
    for c in range(NC):
        c_copies[c].wait_recv()
    multiply_own(0)
    make_signs(1, other_low)
    f_copies[0].wait_recv()
    multiply(0, 0, 0)
    multiply_own(1)
    multiply(0, 0, 1)
    make_signs(2, low)
    forward(1)
    make_signs(2, other_low)
    f_copies[1].wait_recv()
    multiply(1, 1, 0)
    multiply(1, 1, 1)
    combine(0, 0)
    multiply_own(2)
    multiply(0, 1, 2)
    forward(2)
    make_signs(3, low)
    f_copies[2].wait_recv()
    multiply(2, 2, 0)
    multiply(2, 2, 2)
    combine(1, 0)
    multiply(2, 2, 1)
    forward(3)
    make_signs(3, other_low)
    multiply_own(3)
    multiply(0, 2, 3)

    @pl.when(is_mid)
    def _():
        pl.semaphore_wait(ready, 1)

    combine(0, 1)
    combine(1, 1)
    forward(4)
    f_copies[3].wait_recv()
    multiply(3, 3, 2)
    multiply(3, 3, 0)
    f_copies[4].wait_recv()
    multiply(4, 4, 2)
    multiply(4, 4, 0)
    combine(2, 0)
    combine(2, 1)
    multiply(3, 4, 3)
    multiply(3, 4, 1)
    combine(3, 1)
    combine(4, 1)
    combine(3, 0)
    combine(4, 0)
    settle(0)
    settle(1)
    settle(2)
    settle(3)
    settle(4)

    whole = feats[...].reshape(2 * ex_rows, width)
    product = lax.dot_general(
        whole, whole, (((1,), (1,)), ((), ())), preferred_element_type=jnp.float32
    ) * (1.0 / math.sqrt(K))
    for half in range(2):
        columns = product[:, half * 128 : (half + 1) * 128].astype(jnp.bfloat16)
        kout[half] = columns.reshape(8, 32, 128)

    def k_copy(k):
        target = lax.rem(me + k, 16)
        return remote(
            kout.at[target % 2, target // 2], kin.at[k], k_send.at[k], k_recv.at[k], at_offset(k)
        )

    for k in range(1, 16):
        k_copy(k).start()
    feat_ref[:, pl.ds(pl.multiple_of(ex * width, width), width)] = feats[ex]
    key_copy.wait_send()
    for c in range(NC):
        g_copies[c].wait_send()
        c_copies[c].wait_send()
        f_copies[c].wait_send()
        y_copy(c, 0).wait_send()
        y_copy(c, 1).wait_send()
        z_copy(c, 1).wait_send()

    @pl.when(is_mid)
    def _():
        for c in range(NC):
            z_copy(c, 0).wait_send()

    for c in range(NC):
        fx_copy(c).wait_recv()
        fx_copy(c).wait_send()
    feat_ref[:, pl.ds(pl.multiple_of(other_ex * width, width), width)] = feats_in[...]
    total = kout[ex, par].astype(jnp.float32)
    for k in range(1, 16):
        k_copy(k).wait_recv()
        total += kin[k].astype(jnp.float32)
    kern_ref[...] = total

    for k in range(1, 16):
        k_copy(k).wait_send()


def write_kernel(feat_in, kern_in, feat_ref, kern_ref, sems):
    copies = (
        pltpu.make_async_copy(feat_in, feat_ref, sems.at[0]),
        pltpu.make_async_copy(kern_in, kern_ref, sems.at[1]),
    )
    for copy in copies:
        copy.start()
    for copy in copies:
        copy.wait()


def line(gradients, proj_seed, block_keys):
    ex_rows, params = gradients.shape
    width = K // 16
    dma = pltpu.SemaphoreType.DMA
    bf16 = jnp.bfloat16
    pair = pl.pallas_call(
        line_kernel,
        out_shape=(
            jax.ShapeDtypeStruct((ex_rows, K // 8), bf16),
            jax.ShapeDtypeStruct((2 * ex_rows // 8, ex_rows), jnp.float32),
        ),
        in_specs=[
            pl.BlockSpec(memory_space=pltpu.SMEM),
            pl.BlockSpec(memory_space=pltpu.HBM),
            pl.BlockSpec(memory_space=pltpu.HBM),
        ],
        out_specs=(
            pl.BlockSpec(memory_space=pltpu.VMEM),
            pl.BlockSpec(memory_space=pltpu.VMEM),
        ),
        scratch_shapes=[
            pltpu.VMEM((2, 2 * ex_rows, params), bf16),
            pltpu.VMEM((STEPS, 2, params, width), bf16),
            pltpu.VMEM((2, params, 128), jnp.int32),
            pltpu.VMEM((2,) + block_keys.shape, jnp.int32),
            pltpu.VMEM((STEPS, 2 * ex_rows, width), jnp.float32),
            pltpu.VMEM((2, 2 * ex_rows, width), bf16),
            pltpu.VMEM((2, 2 * ex_rows, width), bf16),
            pltpu.VMEM((2, 2 * ex_rows, width), bf16),
            pltpu.VMEM((2, 2 * ex_rows, width), bf16),
            pltpu.VMEM((2, ex_rows, width), bf16),
            pltpu.VMEM((ex_rows, width), bf16),
            pltpu.VMEM((2, 8, 32, 128), bf16),
            pltpu.VMEM((16, 32, 128), bf16),
            dma((NC,)),
            dma((NC,)), dma((NC,)), dma((NC,)), dma((NC,)), dma((NC,)), dma((NC,)),
            dma((3,)),
            dma((2, NC)), dma((2, NC)), dma((2, NC)), dma((2, NC)),
            dma((NC,)), dma((NC,)), dma((16,)), dma((16,)), pltpu.SemaphoreType.REGULAR,
        ],
        compiler_params=pltpu.CompilerParams(
            collective_id=0, has_side_effects=True, vmem_limit_bytes=30 * 1024 * 1024
        ),
    )(proj_seed, *(pltpu.with_memory_space_constraint(a, pltpu.HBM) for a in (block_keys, gradients)))
    return pl.pallas_call(
        write_kernel,
        out_shape=tuple(jax.ShapeDtypeStruct(part.shape, part.dtype) for part in pair),
        in_specs=[pl.BlockSpec(memory_space=pltpu.VMEM)] * 2,
        out_specs=(pl.BlockSpec(memory_space=pltpu.HBM),) * 2,
        scratch_shapes=[dma((2,))],
        compiler_params=pltpu.CompilerParams(vmem_limit_bytes=1024 * 1024),
    )(*pair)


def solution(mesh):
    placed = (P(("grp", "ex"), "par"), P(), P(None, "par"))
    special = mesh.shape["par"] == 8 and mesh.shape["ex"] == 2
    return jax.shard_map(
        line if special else general,
        mesh=mesh,
        in_specs=placed,
        out_specs=(P(("grp", "ex"), "par"), P(("grp", "par"), "ex")),
        check_vma=False,
    )
```

```python
import functools
import math

import jax
import jax.numpy as jnp
import numpy as np
from jax import lax
from jax.experimental import pallas as pl
from jax.experimental.pallas import tpu as pltpu
from jax.sharding import PartitionSpec as P

K = 8192
PBLK = 512
MESH = pl.DeviceIdType.MESH
ROW_MUL = 73856093
COL_MUL = 19349663
KEY_MUL = 83492791
MIX_MUL = int(np.array((1540483477 << 5) & 0xFFFFFFFF, np.uint32).astype(np.int32))

STEPS = 4
TILE = 256
CHUNKS = ((0, 16), (16, 48), (64, 32), (96, 16), (112, 16))
NC = len(CHUNKS)


def rademacher(seed_value, block_key, row_index, col_index):
    mixed = row_index * 73856093 ^ col_index * 19349663 ^ block_key * 83492791 ^ seed_value
    mixed = mixed ^ mixed >> 13 & 524287
    mixed = mixed * 1540483477
    mixed = mixed ^ mixed >> 15 & 131071
    parity = mixed >> 11 & 1
    return (1 - 2 * parity).astype(jnp.bfloat16)


def project(slab, key_row, row_base, seed_value, col_index):
    block_count = slab.shape[1] // PBLK
    local_rows = jnp.arange(PBLK, dtype=jnp.int32)[:, None]
    summed = None
    for number in range(block_count):
        sign_block = rademacher(
            seed_value, key_row[number], row_base + number * PBLK + local_rows, col_index
        )
        slab_part = slab[:, number * PBLK : (number + 1) * PBLK]
        product = jnp.dot(slab_part, sign_block, preferred_element_type=jnp.float32)
        summed = product if summed is None else summed + product
    return summed


def general(gradients, proj_seed, block_keys):
    local_params = gradients.shape[1]
    shard_count = lax.axis_size("par")
    shard_index = lax.axis_index("par")
    seed_value = proj_seed[0]
    all_cols = jnp.arange(K, dtype=jnp.int32)[None, :]
    partial_value = project(
        gradients, block_keys[0], shard_index * local_params, seed_value, all_cols
    )
    projected = lax.psum_scatter(
        partial_value.astype(jnp.bfloat16), "par", scatter_dimension=1, tiled=True
    ).astype(jnp.float32)
    features = jnp.tanh(projected * (1.0 / math.sqrt(local_params * shard_count))).astype(
        jnp.bfloat16
    )
    gathered = lax.all_gather(features, "ex", axis=0, tiled=True)
    product = lax.dot_general(
        gathered, features, (((1,), (1,)), ((), ())), preferred_element_type=jnp.float32
    )
    kernel = lax.psum_scatter(
        (product * (1.0 / math.sqrt(K))).astype(jnp.bfloat16),
        "par",
        scatter_dimension=0,
        tiled=True,
    ).astype(jnp.float32)
    return (features, kernel)


def fold(value):
    return value ^ lax.shift_right_logical(value, 13)


def line_kernel(
    seed_ref, key_hbm, g_ref, feat_ref, kern_ref,
    x, signs, rows, keys, acc, yout, yin, zout, zin, feats, feats_in, kout, kin,
    load_sems, g_send, g_recv, c_send, c_recv, f_send, f_recv, key_sems,
    y_send, y_recv, z_send, z_recv, fx_send, fx_recv, k_send, k_recv, ready,
):
    ex_rows, params = g_ref.shape
    width = K // 16
    par, ex = lax.axis_index("par"), lax.axis_index("ex")
    z, y = par // 2, par % 2
    side, low = z // 2, z % 2
    other_y, other_ex, other_low = 1 - y, 1 - ex, 1 - low
    is_end = side == low
    is_mid = jnp.logical_not(is_end)
    me = par * 2 + ex
    blocks = params // PBLK

    half = jnp.where(is_end, side, 1 - side)
    z_cross = jnp.where(is_end, 1 + half, 3 * half)
    z_same = jnp.where(is_end, 3 * half, 1 + half)

    y_dev = {"par": z * 2 + other_y}
    c_dev = {"ex": other_ex}
    pair_dev = {"par": (side * 2 + other_low) * 2 + y}
    far_dev = {"par": (3 - z) * 2 + y}
    cross_dev = {"par": z_cross * 2 + y}

    barrier = pltpu.get_barrier_semaphore()
    pl.semaphore_signal(barrier, inc=1, device_id=y_dev, device_id_type=MESH)
    pl.semaphore_signal(barrier, inc=1, device_id=pair_dev, device_id_type=MESH)
    pl.semaphore_signal(barrier, inc=1, device_id=c_dev, device_id_type=MESH)

    @pl.when(is_mid)
    def _():
        pl.semaphore_signal(barrier, inc=1, device_id=far_dev, device_id_type=MESH)


    def remote(src, dst, send, recv, device):
        return pltpu.make_async_remote_copy(
            src_ref=src, dst_ref=dst, send_sem=send, recv_sem=recv,
            device_id=device, device_id_type=MESH,
        )

    def at_offset(k):
        target = lax.rem(me + k, 16)
        return {"par": target // 2, "ex": target % 2}

    def span(c):
        return slice(2 * CHUNKS[c][0], 2 * (CHUNKS[c][0] + CHUNKS[c][1]))

    def mine(c, core):
        first, count = CHUNKS[c]
        return pl.ds(pl.multiple_of(2 * first + core * count, 16), count)

    loads, g_copies, c_copies, f_copies = [], [], [], []
    for c, (first, count) in enumerate(CHUNKS):
        own = g_ref.at[pl.ds(first, count)]
        here = x.at[low, mine(c, ex)]
        there = x.at[other_low, mine(c, ex)]
        loads.append(
            pltpu.make_async_copy(own, here, load_sems.at[c])
        )
        g_copies.append(remote(here, here, g_send.at[c], g_recv.at[c], pair_dev))
        c_copies.append(remote(here, here, c_send.at[c], c_recv.at[c], c_dev))
        f_copies.append(remote(there, there, f_send.at[c], f_recv.at[c], c_dev))
        loads[c].start()

    local_keys = pltpu.make_async_copy(key_hbm, keys.at[low], key_sems.at[2])
    local_keys.start()
    seed = seed_ref[0]

    def make_rows(which):
        for b in range(blocks):
            index = lax.broadcasted_iota(jnp.int32, (PBLK, 128), 0)
            index = index + (((side * 2 + which) * 2 + y) * params + b * PBLK)
            value = index * ROW_MUL ^ (keys[which, :, b : b + 1] * KEY_MUL ^ seed)
            rows[which, b * PBLK : (b + 1) * PBLK, :] = fold(value)

    def make_signs(step, which):
        owner = (z_same if step < 2 else z_cross) * 2 + (other_y if step % 2 == 0 else y)
        base = owner * (2 * width) + ex * width
        cols = []
        for j in range(width // 128):
            col = lax.broadcasted_iota(jnp.int32, (8, 128), 1) + (base + j * 128)
            cols.append(fold(col * COL_MUL)[:1])

        def body(i, carry):
            start = pl.multiple_of(i * TILE, TILE)
            row = rows[which, pl.ds(start, TILE), :]
            for j, col in enumerate(cols):
                mixed = (row ^ col) * MIX_MUL
                mixed = mixed ^ (mixed << 15)
                sign = jnp.where(mixed < 0, jnp.bfloat16(-1.0), jnp.bfloat16(1.0))
                signs[step, which, pl.ds(start, TILE), j * 128 : (j + 1) * 128] = sign
            return carry

        lax.fori_loop(0, params // TILE, body, 0)

    def multiply_own(s):
        left = x[low]
        for n in range(width // 256):
            cols = slice(n * 256, (n + 1) * 256)
            acc[s, :, cols] = jnp.dot(
                left, signs[s, low, :, cols], preferred_element_type=jnp.float32
            )

    def y_copy(c, kind):
        part = span(c)
        return remote(
            yout.at[kind, part], yin.at[kind, part],
            y_send.at[kind, c], y_recv.at[kind, c], y_dev,
        )

    def z_copy(c, kind):
        part = span(c)
        return remote(
            zout.at[kind, part], zin.at[kind, part], z_send.at[kind, c], z_recv.at[kind, c],
            far_dev if kind == 0 else cross_dev,
        )

    def multiply(first, last, s):
        part = slice(span(first).start, span(last).stop)
        left = x[other_low, part]
        for n in range(width // 256):
            cols = slice(n * 256, (n + 1) * 256)
            total = acc[s, part, cols] + jnp.dot(
                left, signs[s, other_low, :, cols], preferred_element_type=jnp.float32
            )
            if s % 2 == 0:
                yout[s // 2, part, cols] = total.astype(jnp.bfloat16)
            else:
                acc[s, part, cols] = total
        if s % 2 == 0:
            for c in range(first, last + 1):
                y_copy(c, s // 2).start()

    def combine(c, kind):
        part = span(c)
        y_copy(c, kind).wait_recv()
        total = acc[2 * kind + 1, part] + yin[kind, part].astype(jnp.float32)
        if kind == 1:
            zout[1, part] = total.astype(jnp.bfloat16)
            z_copy(c, 1).start()
            return

        @pl.when(is_mid)
        def _():
            zout[0, part] = total.astype(jnp.bfloat16)
            z_copy(c, 0).start()

        @pl.when(is_end)
        def _():
            acc[1, part] = total

    scale = 1.0 / math.sqrt(params * 8)

    def fx_copy(c):
        first, count = CHUNKS[c]
        part = pl.ds(first, count)
        return remote(
            feats.at[other_ex, part], feats_in.at[part], fx_send.at[c], fx_recv.at[c], c_dev
        )

    def settle(c):
        first, count = CHUNKS[c]
        part = span(c)
        @pl.when(is_mid)
        def _():
            z_copy(c, 0).wait_recv()
            acc[1, part] = zin[0, part].astype(jnp.float32)

        z_copy(c, 1).wait_recv()
        total = acc[1, part] + zin[1, part].astype(jnp.float32)
        value = jnp.tanh(total * scale).astype(jnp.bfloat16)
        feats[:, first : first + count, :] = value.reshape(2, count, width)
        fx_copy(c).start()

    def forward(c):
        g_copies[c].wait_recv()
        f_copies[c].start()

    @pl.when(is_end)
    def _():
        pl.semaphore_wait(barrier, 3)

    @pl.when(is_mid)
    def _():
        pl.semaphore_wait(barrier, 4)

    key_copy = remote(key_hbm, keys.at[low], key_sems.at[0], key_sems.at[1], pair_dev)
    key_copy.start()
    for c in range(NC):
        loads[c].wait()
        g_copies[c].start()
    for c in range(NC):
        c_copies[c].start()

    @pl.when(is_mid)
    def _():
        pl.semaphore_signal(ready, inc=1, device_id=far_dev, device_id_type=MESH)

    local_keys.wait()
    make_rows(low)
    make_signs(0, low)
    make_signs(1, low)
    key_copy.wait_recv()
    make_rows(other_low)
    make_signs(0, other_low)
    forward(0)
    for c in range(NC):
        c_copies[c].wait_recv()
    multiply_own(0)
    make_signs(1, other_low)
    f_copies[0].wait_recv()
    multiply(0, 0, 0)
    multiply_own(1)
    multiply(0, 0, 1)
    make_signs(2, low)
    forward(1)
    make_signs(2, other_low)
    f_copies[1].wait_recv()
    multiply(1, 1, 0)
    multiply(1, 1, 1)
    combine(0, 0)
    multiply_own(2)
    multiply(0, 1, 2)
    forward(2)
    make_signs(3, low)
    f_copies[2].wait_recv()
    multiply(2, 2, 0)
    multiply(2, 2, 2)
    combine(1, 0)
    multiply(2, 2, 1)
    forward(3)
    make_signs(3, other_low)
    multiply_own(3)
    multiply(0, 2, 3)

    @pl.when(is_mid)
    def _():
        pl.semaphore_wait(ready, 1)

    combine(0, 1)
    combine(1, 1)
    forward(4)
    f_copies[3].wait_recv()
    multiply(3, 3, 2)
    multiply(3, 3, 0)
    f_copies[4].wait_recv()
    multiply(4, 4, 2)
    multiply(4, 4, 0)
    combine(2, 0)
    combine(2, 1)
    multiply(3, 4, 3)
    multiply(3, 4, 1)
    combine(3, 1)
    combine(4, 1)
    combine(3, 0)
    combine(4, 0)
    settle(0)
    settle(1)
    settle(2)
    settle(3)
    settle(4)

    whole = feats[...].reshape(2 * ex_rows, width)
    product = lax.dot_general(
        whole, whole, (((1,), (1,)), ((), ())), preferred_element_type=jnp.float32
    ) * (1.0 / math.sqrt(K))
    for half in range(2):
        columns = product[:, half * 128 : (half + 1) * 128].astype(jnp.bfloat16)
        kout[half] = columns.reshape(8, 32, 128)

    def k_copy(k):
        target = lax.rem(me + k, 16)
        return remote(
            kout.at[target % 2, target // 2], kin.at[k], k_send.at[k], k_recv.at[k], at_offset(k)
        )

    for k in range(1, 16):
        k_copy(k).start()
    feat_ref[:, pl.ds(pl.multiple_of(ex * width, width), width)] = feats[ex]
    key_copy.wait_send()
    for c in range(NC):
        g_copies[c].wait_send()
        c_copies[c].wait_send()
        f_copies[c].wait_send()
        y_copy(c, 0).wait_send()
        y_copy(c, 1).wait_send()
        z_copy(c, 1).wait_send()

    @pl.when(is_mid)
    def _():
        for c in range(NC):
            z_copy(c, 0).wait_send()

    for c in range(NC):
        fx_copy(c).wait_recv()
        fx_copy(c).wait_send()
    feat_ref[:, pl.ds(pl.multiple_of(other_ex * width, width), width)] = feats_in[...]
    total = kout[ex, par].astype(jnp.float32)
    for k in range(1, 16):
        k_copy(k).wait_recv()
        total += kin[k].astype(jnp.float32)
    kern_ref[...] = total

    for k in range(1, 16):
        k_copy(k).wait_send()


def write_kernel(feat_in, kern_in, feat_ref, kern_ref, sems):
    copies = (
        pltpu.make_async_copy(feat_in, feat_ref, sems.at[0]),
        pltpu.make_async_copy(kern_in, kern_ref, sems.at[1]),
    )
    for copy in copies:
        copy.start()
    for copy in copies:
        copy.wait()


def line(gradients, proj_seed, block_keys):
    ex_rows, params = gradients.shape
    width = K // 16
    dma = pltpu.SemaphoreType.DMA
    bf16 = jnp.bfloat16
    pair = pl.pallas_call(
        line_kernel,
        out_shape=(
            jax.ShapeDtypeStruct((ex_rows, K // 8), bf16),
            jax.ShapeDtypeStruct((2 * ex_rows // 8, ex_rows), jnp.float32),
        ),
        in_specs=[
            pl.BlockSpec(memory_space=pltpu.SMEM),
            pl.BlockSpec(memory_space=pltpu.HBM),
            pl.BlockSpec(memory_space=pltpu.HBM),
        ],
        out_specs=(
            pl.BlockSpec(memory_space=pltpu.VMEM),
            pl.BlockSpec(memory_space=pltpu.VMEM),
        ),
        scratch_shapes=[
            pltpu.VMEM((2, 2 * ex_rows, params), bf16),
            pltpu.VMEM((STEPS, 2, params, width), bf16),
            pltpu.VMEM((2, params, 128), jnp.int32),
            pltpu.VMEM((2,) + block_keys.shape, jnp.int32),
            pltpu.VMEM((STEPS, 2 * ex_rows, width), jnp.float32),
            pltpu.VMEM((2, 2 * ex_rows, width), bf16),
            pltpu.VMEM((2, 2 * ex_rows, width), bf16),
            pltpu.VMEM((2, 2 * ex_rows, width), bf16),
            pltpu.VMEM((2, 2 * ex_rows, width), bf16),
            pltpu.VMEM((2, ex_rows, width), bf16),
            pltpu.VMEM((ex_rows, width), bf16),
            pltpu.VMEM((2, 8, 32, 128), bf16),
            pltpu.VMEM((16, 32, 128), bf16),
            dma((NC,)),
            dma((NC,)), dma((NC,)), dma((NC,)), dma((NC,)), dma((NC,)), dma((NC,)),
            dma((3,)),
            dma((2, NC)), dma((2, NC)), dma((2, NC)), dma((2, NC)),
            dma((NC,)), dma((NC,)), dma((16,)), dma((16,)), pltpu.SemaphoreType.REGULAR,
        ],
        compiler_params=pltpu.CompilerParams(
            collective_id=0, has_side_effects=True, vmem_limit_bytes=30 * 1024 * 1024
        ),
    )(proj_seed, *(pltpu.with_memory_space_constraint(a, pltpu.HBM) for a in (block_keys, gradients)))
    return pl.pallas_call(
        write_kernel,
        out_shape=tuple(jax.ShapeDtypeStruct(part.shape, part.dtype) for part in pair),
        in_specs=[pl.BlockSpec(memory_space=pltpu.VMEM)] * 2,
        out_specs=(pl.BlockSpec(memory_space=pltpu.HBM),) * 2,
        scratch_shapes=[dma((2,))],
        compiler_params=pltpu.CompilerParams(vmem_limit_bytes=1024 * 1024),
    )(*pair)


def solution(mesh):
    placed = (P(("grp", "ex"), "par"), P(), P(None, "par"))
    special = mesh.shape["par"] == 8 and mesh.shape["ex"] == 2
    return jax.shard_map(
        line if special else general,
        mesh=mesh,
        in_specs=placed,
        out_specs=(P(("grp", "ex"), "par"), P(("grp", "par"), "ex")),
        check_vma=False,
    )
```
